256 devices in a mesh: pair: 64 (over x, z, core), fac: 4 (over y).
Axes of the slice: x: 4, y: 4, z: 8, core: 2. Of those that a mesh axis runs over, the one named last changes fastest.
Arguments:
- amplitudes: bfloat16 [256, 1024, 1024], P(('pair', 'fac')), may hold values from -6 to 6
- mirror_slot: int32 [256], P(('pair', 'fac')), may hold values from 0 to 0, as said below
- d_values: bfloat16 [4, 16, 64, 64], P('fac'), may hold values from -0.375 to 0.375
- d_cols: int32 [4, 16], P('fac'), may hold values from 0 to 15
- b_values: bfloat16 [4, 16, 64, 64], P('fac'), may hold values from -0.375 to 0.375
- b_cols: int32 [4, 16], P('fac'), may hold values from 0 to 15
Outputs:
- residual: bfloat16 [256, 1024, 1024], P(('pair', 'fac'))
The draws below stay inside these ranges and needn't reach their ends.
Inputs may be any that keep to these rules, and one draw needn't show every extreme that they name: Mirrors are mutual: the pairs on device pair index p and fac index f have their mirrors on pair index (p + 64/2) mod 64 with the same fac index, and m(m(n)) = n; on each device mirror_slot is a permutation of its 1 slots.
All inputs are finite; a program needn't handle non-finite values.
Results may differ from the reference program's by a relative error of at most 0.0059.
Values may be sent and summed in bfloat16 or wider, within the bound.
A program may use at most 128 MiB of HBM per device.

```python
import jax
import jax.numpy as jnp
from jax import lax

V = 1024
BS = 64
Q = 4
PAIR_DEV = 1
NBLK = 16
PAIRS = 256
N_PAIR = 64
N_FAC = 4


def draw_mirror_slot(key, part):
    half = N_PAIR // 2
    scores = jax.random.randint(key, (half, N_FAC, PAIR_DEV), 0, 1 << 20) * PAIR_DEV
    scores = scores + jnp.arange(PAIR_DEV, dtype=jnp.int32)
    forward = jnp.argsort(scores, axis=-1).astype(jnp.int32)
    backward = jnp.argsort(forward, axis=-1).astype(jnp.int32)
    joined = jnp.concatenate([forward, backward], axis=0)
    return joined.reshape(PAIRS).astype(jnp.int32)


def plant(array, key, low, largest):
    place = [jax.random.randint(jax.random.fold_in(key, axis), (), 0, length) for axis, length in enumerate(array.shape)]
    longest = array.shape.index(max(array.shape))
    beside = place[:longest] + [(place[longest] + 1) % array.shape[longest]] + place[longest + 1:]
    return array.at[tuple(place)].set(low).at[tuple(beside)].set(largest)


def block_scale(stream_key, dims, shards, smallest, top_value):
    loudness = 1.0
    for dim, parts in shards:
        steps = jax.random.uniform(jax.random.fold_in(jax.random.fold_in(stream_key, 6), dim), (parts,), jnp.float32, smallest / len(shards), top_value / len(shards))
        loudness = loudness * jnp.repeat(jnp.exp(steps), dims[dim] // parts).reshape((-1,) + (1,) * (len(dims) - 1 - dim))
    return loudness


def scatter_about(stream_key, shape, width, limit, split=(), kind=jnp.bfloat16):
    array = width * jax.random.normal(stream_key, shape, jnp.float32)
    if split:
        array = array * block_scale(stream_key, shape, split, -0.22, 0.18)
    return jnp.clip(array, -limit, limit).astype(kind)


def setup_inputs(seed: int = 0) -> dict:
    splits = jax.random.split(jax.random.key(seed), 7)
    amplitudes = scatter_about(splits[0], (PAIRS, V, V), 1.0, 6.0, ((0, 256),))
    mirror_slot = draw_mirror_slot(jax.random.fold_in(splits[6], 71), 0)
    d_values = scatter_about(splits[2], (Q, NBLK, BS, BS), (4 * BS) ** -0.5, 0.375, ((0, 4),))
    d_cols = plant(jax.random.randint(splits[3], (Q, NBLK), 0, NBLK), jax.random.fold_in(splits[3], 1), 0, NBLK - 1).astype(jnp.int32)
    b_values = scatter_about(splits[4], (Q, NBLK, BS, BS), (4 * BS) ** -0.5, 0.375, ((0, 4),))
    b_cols = plant(jax.random.randint(splits[5], (Q, NBLK), 0, NBLK), jax.random.fold_in(splits[5], 1), 0, NBLK - 1).astype(jnp.int32)
    return {"amplitudes": amplitudes, "mirror_slot": mirror_slot, "d_values": d_values, "d_cols": d_cols, "b_values": b_values, "b_cols": b_cols}


def dress_one(amps, d_values, d_cols, b_values, b_cols):
    total = jnp.zeros((V, V), jnp.float32)
    for factor in range(Q):
        blocks = amps.reshape(NBLK, BS, V)
        picked = jnp.take(blocks, d_cols[factor], axis=0)
        left = jnp.einsum('rab,rbv->rav', d_values[factor].astype(jnp.float32), picked.astype(jnp.float32))
        left = left.reshape(V, V).astype(jnp.bfloat16)
        columns = left.reshape(V, NBLK, BS)
        chosen = jnp.take(columns, b_cols[factor], axis=1)
        right = jnp.einsum('arb,rcb->arc', chosen.astype(jnp.float32), b_values[factor].astype(jnp.float32))
        total = total + right.reshape(V, V)
    return total.astype(jnp.bfloat16)


def reference(amplitudes, mirror_slot, d_values, d_cols, b_values, b_cols):
    dressed = lax.map(lambda amps: dress_one(amps, d_values, d_cols, b_values, b_cols), amplitudes)
    index = jnp.arange(PAIRS, dtype=jnp.int32)
    device = index // PAIR_DEV
    pair_pos = device // N_FAC
    fac_pos = device % N_FAC
    partner = ((pair_pos + N_PAIR // 2) % N_PAIR * N_FAC + fac_pos) * PAIR_DEV + mirror_slot
    partner = partner.astype(jnp.int32)

    def finish(which):
        own = lax.dynamic_index_in_dim(dressed, which, 0, keepdims=False)
        other = lax.dynamic_index_in_dim(dressed, partner[which], 0, keepdims=False)
        return (own.astype(jnp.float32) + other.astype(jnp.float32).T).astype(jnp.bfloat16)

    return lax.map(finish, index)
```

```python
import jax
import jax.numpy as jnp
from jax import lax
from jax.experimental import pallas as pl
from jax.experimental.pallas import tpu as pltpu
from jax.sharding import PartitionSpec as P

MESH = pl.DeviceIdType.MESH
F32 = jnp.float32
BF16 = jnp.bfloat16
LANES = 128
GROUP = 256
NT = (((1,), (1,)), ((), ()))


def make_kernel(n_pair, n_fac, v, bs):
    nblk = v // bs
    chunks = v // LANES
    groups = v // GROUP
    per = GROUP // bs
    half = n_pair // 2

    def kernel(
        t_ref, slot_ref, d_ref, dcol_ref, b_ref, bcol_ref, out_ref,
        own_t, mirror_t, work_t, slot_s, d_land, b_land, dc_land, bc_land, dc_s, bc_s,
        d_diag, b_dense, left, left_k, acc, own_x,
        t_send, t_recv, f_send, f_recv, local_sem,
    ):
        p = lax.axis_index("pair")
        f = lax.axis_index("fac")
        mirror = (lax.rem(p + half, n_pair), f)

        def fac_peer(k):
            return (p, lax.rem(f + n_fac - k, n_fac))

        barrier = pltpu.get_barrier_semaphore()
        pl.semaphore_signal(barrier, inc=1, device_id=mirror, device_id_type=MESH)
        for k in range(1, n_fac):
            pl.semaphore_signal(barrier, inc=1, device_id=fac_peer(k), device_id_type=MESH)

        factors = ((d_ref, d_land), (dcol_ref, dc_land), (b_ref, b_land), (bcol_ref, bc_land))
        loads = [pltpu.make_async_copy(src, dst.at[0], local_sem.at[i]) for i, (src, dst) in enumerate(factors)]
        loads.append(pltpu.make_async_copy(t_ref, own_t, local_sem.at[4]))
        loads.append(pltpu.make_async_copy(slot_ref, slot_s, local_sem.at[5]))
        for load in loads:
            load.start()

        pl.semaphore_wait(barrier, n_fac)

        sends = []
        for k in range(1, n_fac):
            for i, (src, dst) in enumerate(factors):
                sends.append(pltpu.make_async_remote_copy(
                    src_ref=src, dst_ref=dst.at[k], send_sem=f_send.at[k, i], recv_sem=f_recv.at[k, i],
                    device_id=fac_peer(k), device_id_type=MESH))
        for j in range(chunks):
            sends.append(pltpu.make_async_remote_copy(
                src_ref=t_ref.at[:, :, pl.ds(j * LANES, LANES)], dst_ref=mirror_t.at[j],
                send_sem=t_send.at[j], recv_sem=t_recv.at[j], device_id=mirror, device_id_type=MESH))
        for send in sends:
            send.start()

        acc[...] = jnp.zeros_like(acc)
        rows_i = lax.broadcasted_iota(jnp.int32, (bs, LANES), 0)
        lanes_i = lax.broadcasted_iota(jnp.int32, (bs, LANES), 1)
        twice = jnp.where(lax.rem(lanes_i, bs) == rows_i, 1.0, 0.0).astype(BF16)
        which = lanes_i // bs

        for load in loads:
            load.wait()

        for k in range(n_fac):
            if k > 0:
                for send in sends[4 * (k - 1):4 * k]:
                    send.wait_recv()
            for i, (land, small) in enumerate(((dc_land, dc_s), (bc_land, bc_s))):
                move = pltpu.make_async_copy(land.at[k], small.at[k], local_sem.at[6 + i])
                move.start()
                move.wait()

            def build_d(g, _):
                rows = pl.ds(pl.multiple_of(g * GROUP, GROUP), GROUP)
                pair = jnp.dot(d_land[k, rows, :], twice, preferred_element_type=F32)
                for i in range(per):
                    part = pair[i * bs:(i + 1) * bs, :]
                    to = pl.ds(pl.multiple_of(g * GROUP + i * bs, bs), bs)
                    for h in range(GROUP // LANES):
                        piece = jnp.where(which + (LANES // bs) * h == i, part, 0.0)
                        d_diag[k, to, h * LANES:(h + 1) * LANES] = piece.astype(BF16)
                return 0

            lax.fori_loop(0, groups, build_d, 0)

            def build_b(c, _):
                rows = pl.ds(pl.multiple_of(c * bs, bs), bs)
                part = jnp.dot(b_land[k, rows, :], twice, preferred_element_type=F32)
                col = bc_s[k, 0, c]
                for j in range(chunks):
                    piece = jnp.where(which + (LANES // bs) * j == col, part, 0.0)
                    b_dense[j, rows, k * LANES:(k + 1) * LANES] = piece.astype(BF16)
                return 0

            lax.fori_loop(0, nblk, build_b, 0)

            def own_left(g, _):
                rows = pl.ds(pl.multiple_of(g * GROUP, GROUP), GROUP)
                picked = jnp.concatenate(
                    [own_t[dc_s[k, 0, g * per + i]] for i in range(per)], axis=0)
                left[rows, :] = jnp.dot(d_diag[k, rows, :], picked, preferred_element_type=F32).astype(BF16)
                return 0

            lax.fori_loop(0, groups, own_left, 0)

            def own_right(n, _):
                rows = pl.ds(pl.multiple_of(n * GROUP, GROUP), GROUP)
                right = jnp.concatenate([b_dense[j, rows, k * LANES:(k + 1) * LANES] for j in range(chunks)], axis=1)
                acc[:, rows] += lax.dot_general(left[...], right, NT, preferred_element_type=F32)
                return 0

            lax.fori_loop(0, groups, own_right, 0)

        own_x[...] = acc[...].astype(BF16)
        acc[...] = jnp.zeros_like(acc)
        base = slot_s[0] * nblk

        def mirror_left(j):
            work_t[...] = mirror_t[j]
            for k in range(n_fac):
                for g in range(groups):
                    rows = slice(g * GROUP, (g + 1) * GROUP)
                    picked = jnp.concatenate(
                        [work_t[base + dc_s[k, 0, g * per + i]] for i in range(per)], axis=0)
                    left_k[rows, k * LANES:(k + 1) * LANES] = jnp.dot(
                        d_diag[k, rows, :], picked, preferred_element_type=F32).astype(BF16)

        def mirror_step(j, _):
            pltpu.make_async_remote_copy(
                src_ref=t_ref.at[:, :, pl.ds(0, LANES)], dst_ref=mirror_t.at[j],
                send_sem=t_send.at[j], recv_sem=t_recv.at[j], device_id=mirror, device_id_type=MESH).wait_recv()
            mirror_left(j)
            acc[...] += lax.dot_general(b_dense[j], left_k[...], NT, preferred_element_type=F32)
            return 0

        lax.fori_loop(0, chunks - 1, mirror_step, 0)
        sends[-1].wait_recv()
        mirror_left(chunks - 1)
        other = acc[...] + lax.dot_general(b_dense[chunks - 1], left_k[...], NT, preferred_element_type=F32)
        out_ref[...] = (own_x[...].astype(F32) + other.astype(BF16).astype(F32)).astype(BF16)
        for send in sends:
            send.wait_send()

    return kernel


def shards(amplitudes, mirror_slot, d_values, d_cols, b_values, b_cols):
    n_pair, n_fac = lax.axis_size("pair"), lax.axis_size("fac")
    v = amplitudes.shape[1]
    bs = d_values.shape[-1]
    nblk = v // bs
    chunks = v // LANES
    anywhere = pl.BlockSpec(memory_space=pltpu.HBM)
    out = pl.pallas_call(
        make_kernel(n_pair, n_fac, v, bs),
        out_shape=pltpu.VMEM((v, v), BF16),
        in_specs=[anywhere] * 6,
        out_specs=pl.BlockSpec(memory_space=pltpu.VMEM),
        scratch_shapes=[
            pltpu.VMEM((nblk, bs, v), BF16),
            pltpu.VMEM((chunks, nblk, bs, LANES), BF16),
            pltpu.VMEM((nblk, bs, LANES), BF16),
            pltpu.SMEM((1,), jnp.int32),
            pltpu.VMEM((n_fac, v, bs), BF16),
            pltpu.VMEM((n_fac, v, bs), BF16),
            pltpu.VMEM((n_fac, 1, nblk), jnp.int32),
            pltpu.VMEM((n_fac, 1, nblk), jnp.int32),
            pltpu.SMEM((n_fac, 1, nblk), jnp.int32),
            pltpu.SMEM((n_fac, 1, nblk), jnp.int32),
            pltpu.VMEM((n_fac, v, GROUP), BF16),
            pltpu.VMEM((chunks, v, n_fac * LANES), BF16),
            pltpu.VMEM((v, v), BF16),
            pltpu.VMEM((v, n_fac * LANES), BF16),
            pltpu.VMEM((v, v), F32),
            pltpu.VMEM((v, v), BF16),
            pltpu.SemaphoreType.DMA((chunks,)),
            pltpu.SemaphoreType.DMA((chunks,)),
            pltpu.SemaphoreType.DMA((n_fac, 4)),
            pltpu.SemaphoreType.DMA((n_fac, 4)),
            pltpu.SemaphoreType.DMA((8,)),
        ],
        compiler_params=pltpu.CompilerParams(
            collective_id=0, has_side_effects=True, vmem_limit_bytes=56 * 2**20),
        name="ladder",
    )(
        amplitudes.reshape(nblk, bs, v), mirror_slot, d_values.reshape(v, bs), d_cols,
        b_values.reshape(v, bs), b_cols,
    )
    return out[None]


def solution(mesh):
    placed = (
        P(("pair", "fac"), None, None),
        P(("pair", "fac")),
        P("fac", None, None, None),
        P("fac", None),
        P("fac", None, None, None),
        P("fac", None),
    )
    return jax.shard_map(
        shards,
        mesh=mesh,
        in_specs=placed,
        out_specs=P(("pair", "fac"), None, None),
        check_vma=False,
    )
```

```python
import jax
import jax.numpy as jnp
from jax import lax
from jax.experimental import pallas as pl
from jax.experimental.pallas import tpu as pltpu
from jax.sharding import PartitionSpec as P

MESH = pl.DeviceIdType.MESH
F32 = jnp.float32
BF16 = jnp.bfloat16
LANES = 128
GROUP = 256
NT = (((1,), (1,)), ((), ()))


def make_kernel(n_pair, n_fac, v, bs):
    nblk = v // bs
    chunks = v // LANES
    groups = v // GROUP
    per = GROUP // bs
    half = n_pair // 2

    def kernel(
        t_ref, d_ref, dcol_ref, b_ref, bcol_ref, out_ref,
        own_t, mirror_t, work_t, d_in, b_in, land, dc_land, bc_land, dc_s, bc_s,
        d_diag, b_dense, left, left_k, acc, own_x,
        t_send, t_recv, f_send, f_recv, g_send, local_sem,
    ):
        p = lax.axis_index("pair")
        f = lax.axis_index("fac")
        mirror = (lax.rem(p + half, n_pair), f)

        def fac_peer(k):
            return (p, lax.rem(f + n_fac - k, n_fac))

        core = lax.rem(p, 2)
        sibling = (p + 1 - 2 * core, f)
        hub = core == 0

        barrier = pltpu.get_barrier_semaphore()
        pl.semaphore_signal(barrier, inc=1, device_id=mirror, device_id_type=MESH)

        @pl.when(hub)
        def _():
            for k in range(1, n_fac):
                pl.semaphore_signal(barrier, inc=1, device_id=fac_peer(k), device_id_type=MESH)

        @pl.when(core == 1)
        def _():
            pl.semaphore_signal(barrier, inc=1, device_id=sibling, device_id_type=MESH)

        pairs = ((d_ref, d_in), (b_ref, b_in), (dcol_ref, dc_land.at[0]), (bcol_ref, bc_land.at[0]),
                 (t_ref, own_t))
        loads = [pltpu.make_async_copy(src, dst, local_sem.at[i]) for i, (src, dst) in enumerate(pairs)]
        for load in loads:
            load.start()

        lower = lax.broadcasted_iota(jnp.int32, (bs, LANES), 1) - lax.broadcasted_iota(jnp.int32, (bs, LANES), 0)
        to_low = jnp.where(lower == 0, 1.0, 0.0).astype(BF16)
        to_high = jnp.where(lower == bs, 1.0, 0.0).astype(BF16)
        from_i = lax.broadcasted_iota(jnp.int32, (LANES, GROUP), 0)
        to_i = lax.broadcasted_iota(jnp.int32, (LANES, GROUP), 1)
        spread = jnp.where(to_i // LANES * bs + lax.rem(to_i, bs) == from_i, 1.0, 0.0).astype(BF16)
        which = lax.broadcasted_iota(jnp.int32, (16, LANES), 1) // bs
        mid = v // 2

        def mask(hit):
            return jnp.concatenate([jnp.where(hit, 1.0, 0.0).astype(BF16)] * (bs // 16), axis=0)

        for i, ref in enumerate((d_in, b_in)):
            loads[i].wait()
            low = jnp.dot(ref[0:mid, :], to_low, preferred_element_type=F32)
            high = jnp.dot(ref[mid:v, :], to_high, preferred_element_type=F32)
            land[0, i] = (low + high).astype(BF16)

        @pl.when(hub)
        def _():
            pl.semaphore_wait(barrier, n_fac + 1)

        @pl.when(core == 1)
        def _():
            pl.semaphore_wait(barrier, 1)

        t_sends = [
            pltpu.make_async_remote_copy(
                src_ref=t_ref.at[:, :, pl.ds(j * LANES, LANES)], dst_ref=mirror_t.at[j],
                send_sem=t_send.at[j], recv_sem=t_recv.at[j], device_id=mirror, device_id_type=MESH)
            for j in range(chunks)
        ]
        order = [1, n_fac - 1] + list(range(2, n_fac - 1))
        f_sends = {
            k: [
                pltpu.make_async_remote_copy(
                    src_ref=src, dst_ref=dst.at[k], send_sem=f_send.at[k, i], recv_sem=f_recv.at[k, i],
                    device_id=fac_peer(k), device_id_type=MESH)
                for i, (src, dst) in enumerate(((dcol_ref, dc_land), (bcol_ref, bc_land), (land.at[0], land)))
            ]
            for k in order
        }
        passes = {
            k: [
                pltpu.make_async_remote_copy(
                    src_ref=dst.at[k], dst_ref=dst.at[k], send_sem=g_send.at[k, i], recv_sem=f_recv.at[k, i],
                    device_id=sibling, device_id_type=MESH)
                for i, dst in enumerate((dc_land, bc_land, land))
            ]
            for k in order
        }

        t_sends[0].start()

        @pl.when(hub)
        def _():
            for k in order:
                for send in f_sends[k]:
                    send.start()

        for send in t_sends[1:]:
            send.start()

        def receive(k):
            for send in f_sends[k]:
                send.wait_recv()

            @pl.when(hub)
            def _():
                for send in passes[k]:
                    send.start()

        for load in loads[2:]:
            load.wait()

        for step, k in enumerate([0] + order):
            if step == 1:
                receive(order[0])
                receive(order[1])
            elif step == 2:
                for other in order[2:]:
                    receive(other)
            moves = [
                pltpu.make_async_copy(src.at[k], dst.at[k], local_sem.at[5 + i])
                for i, (src, dst) in enumerate(((dc_land, dc_s), (bc_land, bc_s)))
            ]
            for move in moves:
                move.start()

            twice = jnp.dot(land[k, 0], spread, preferred_element_type=F32).astype(BF16)
            none = jnp.zeros((bs, LANES), BF16)
            for r in range(nblk):
                h, i = divmod(r * bs, mid)
                part = twice[i:i + bs, h * LANES:(h + 1) * LANES]
                at = r % per * bs // LANES
                for side in range(GROUP // LANES):
                    piece = part * mask(which == r * bs % LANES // bs) if side == at else none
                    d_diag[k, r * bs:(r + 1) * bs, side * LANES:(side + 1) * LANES] = piece

            for move in moves:
                move.wait()
            twice = jnp.dot(land[k, 1], spread, preferred_element_type=F32).astype(BF16)
            for c in range(nblk):
                h, i = divmod(c * bs, mid)
                part = twice[i:i + bs, h * LANES:(h + 1) * LANES]
                col = bc_s[k, 0, c]
                for j in range(chunks):
                    piece = part * mask(which + (LANES // bs) * j == col)
                    b_dense[j, c * bs:(c + 1) * bs, k * LANES:(k + 1) * LANES] = piece

            for g in range(groups):
                rows = slice(g * GROUP, (g + 1) * GROUP)
                picked = jnp.concatenate([own_t[dc_s[k, 0, g * per + i]] for i in range(per)], axis=0)
                left[rows, :] = jnp.dot(d_diag[k, rows, :], picked, preferred_element_type=F32).astype(BF16)

            right = jnp.concatenate([b_dense[j, :, k * LANES:(k + 1) * LANES] for j in range(chunks)], axis=1)
            part = lax.dot_general(left[...], right, NT, preferred_element_type=F32)
            if step == 0:
                acc[...] = part
            elif step < n_fac - 1:
                acc[...] += part
            else:
                own_x[...] = (acc[...] + part).astype(BF16)

        def mirror_part(j):
            work_t[...] = mirror_t[j]
            for k in range(n_fac):
                for g in range(groups):
                    rows = slice(g * GROUP, (g + 1) * GROUP)
                    picked = jnp.concatenate([work_t[dc_s[k, 0, g * per + i]] for i in range(per)], axis=0)
                    left_k[rows, k * LANES:(k + 1) * LANES] = jnp.dot(
                        d_diag[k, rows, :], picked, preferred_element_type=F32).astype(BF16)
            return lax.dot_general(b_dense[j], left_k[...], NT, preferred_element_type=F32)

        t_sends[0].wait_recv()
        acc[...] = mirror_part(0)

        def mirror_step(j, _):
            pltpu.make_async_remote_copy(
                src_ref=t_ref.at[:, :, pl.ds(0, LANES)], dst_ref=mirror_t.at[j],
                send_sem=t_send.at[j], recv_sem=t_recv.at[j], device_id=mirror, device_id_type=MESH).wait_recv()
            acc[...] += mirror_part(j)
            return 0

        lax.fori_loop(1, chunks - 1, mirror_step, 0)
        t_sends[-1].wait_recv()
        other = (acc[...] + mirror_part(chunks - 1)).astype(BF16)
        out_ref[...] = (own_x[...].astype(F32) + other.astype(F32)).astype(BF16)
        for send in t_sends:
            send.wait_send()

        @pl.when(hub)
        def _():
            for k in order:
                for send in f_sends[k] + passes[k]:
                    send.wait_send()

    return kernel


def shards(amplitudes, mirror_slot, d_values, d_cols, b_values, b_cols):
    n_pair, n_fac = lax.axis_size("pair"), lax.axis_size("fac")
    v = amplitudes.shape[1]
    bs = d_values.shape[-1]
    nblk = v // bs
    chunks = v // LANES
    anywhere = pl.BlockSpec(memory_space=pltpu.HBM)
    out = pl.pallas_call(
        make_kernel(n_pair, n_fac, v, bs),
        out_shape=pltpu.VMEM((v, v), BF16),
        in_specs=[anywhere] * 5,
        out_specs=pl.BlockSpec(memory_space=pltpu.VMEM),
        scratch_shapes=[
            pltpu.VMEM((nblk, bs, v), BF16),
            pltpu.VMEM((chunks, nblk, bs, LANES), BF16),
            pltpu.VMEM((nblk, bs, LANES), BF16),
            pltpu.VMEM((v, bs), BF16),
            pltpu.VMEM((v, bs), BF16),
            pltpu.VMEM((n_fac, 2, v // 2, LANES), BF16),
            pltpu.VMEM((n_fac, 1, nblk), jnp.int32),
            pltpu.VMEM((n_fac, 1, nblk), jnp.int32),
            pltpu.SMEM((n_fac, 1, nblk), jnp.int32),
            pltpu.SMEM((n_fac, 1, nblk), jnp.int32),
            pltpu.VMEM((n_fac, v, GROUP), BF16),
            pltpu.VMEM((chunks, v, n_fac * LANES), BF16),
            pltpu.VMEM((v, v), BF16),
            pltpu.VMEM((v, n_fac * LANES), BF16),
            pltpu.VMEM((v, v), F32),
            pltpu.VMEM((v, v), BF16),
            pltpu.SemaphoreType.DMA((chunks,)),
            pltpu.SemaphoreType.DMA((chunks,)),
            pltpu.SemaphoreType.DMA((n_fac, 3)),
            pltpu.SemaphoreType.DMA((n_fac, 3)),
            pltpu.SemaphoreType.DMA((n_fac, 3)),
            pltpu.SemaphoreType.DMA((7,)),
        ],
        compiler_params=pltpu.CompilerParams(
            collective_id=0, has_side_effects=True, vmem_limit_bytes=56 * 2**20),
        name="ladder",
    )(
        amplitudes.reshape(nblk, bs, v), d_values.reshape(v, bs), d_cols,
        b_values.reshape(v, bs), b_cols,
    )
    return jnp.take(out[None], mirror_slot, axis=0, mode="clip")


def solution(mesh):
    placed = (
        P(("pair", "fac"), None, None),
        P(("pair", "fac")),
        P("fac", None, None, None),
        P("fac", None),
        P("fac", None, None, None),
        P("fac", None),
    )
    return jax.shard_map(
        shards,
        mesh=mesh,
        in_specs=placed,
        out_specs=P(("pair", "fac"), None, None),
        check_vma=False,
    )
```

```python
import jax
import jax.numpy as jnp
from jax import lax
from jax.experimental import pallas as pl
from jax.experimental.pallas import tpu as pltpu
from jax.sharding import PartitionSpec as P

MESH = pl.DeviceIdType.MESH
F32 = jnp.float32
BF16 = jnp.bfloat16
LANES = 128
GROUP = 256
NT = (((1,), (1,)), ((), ()))


def make_kernel(n_pair, n_fac, v, bs):
    nblk = v // bs
    chunks = v // LANES
    groups = v // GROUP
    per = GROUP // bs
    half = n_pair // 2

    def kernel(
        t_ref, d_ref, dcol_ref, b_ref, bcol_ref, acc, left_k, b_last,
        own_t, mirror_t, work_t, last_t, d_in, b_in, land, dc_land, bc_land, dc_s, bc_s,
        d_diag, b_dense, left,
        t_send, t_recv, f_send, f_recv, g_send, local_sem,
    ):
        p = lax.axis_index("pair")
        f = lax.axis_index("fac")
        mirror = (lax.rem(p + half, n_pair), f)

        def fac_peer(k):
            return (p, lax.rem(f + n_fac - k, n_fac))

        core = lax.rem(p, 2)
        sibling = (p + 1 - 2 * core, f)
        hub = core == 0

        barrier = pltpu.get_barrier_semaphore()
        pl.semaphore_signal(barrier, inc=1, device_id=mirror, device_id_type=MESH)

        @pl.when(hub)
        def _():
            for k in range(1, n_fac):
                pl.semaphore_signal(barrier, inc=1, device_id=fac_peer(k), device_id_type=MESH)

        @pl.when(core == 1)
        def _():
            pl.semaphore_signal(barrier, inc=1, device_id=sibling, device_id_type=MESH)

        pairs = ((d_ref, d_in), (b_ref, b_in), (dcol_ref, dc_land.at[0]), (bcol_ref, bc_land.at[0]),
                 (t_ref, own_t))
        loads = [pltpu.make_async_copy(src, dst, local_sem.at[i]) for i, (src, dst) in enumerate(pairs)]
        for load in loads:
            load.start()

        lower = lax.broadcasted_iota(jnp.int32, (bs, LANES), 1) - lax.broadcasted_iota(jnp.int32, (bs, LANES), 0)
        to_low = jnp.where(lower == 0, 1.0, 0.0).astype(BF16)
        to_high = jnp.where(lower == bs, 1.0, 0.0).astype(BF16)
        from_i = lax.broadcasted_iota(jnp.int32, (LANES, GROUP), 0)
        to_i = lax.broadcasted_iota(jnp.int32, (LANES, GROUP), 1)
        spread = jnp.where(to_i // LANES * bs + lax.rem(to_i, bs) == from_i, 1.0, 0.0).astype(BF16)
        which = lax.broadcasted_iota(jnp.int32, (16, LANES), 1) // bs
        mid = v // 2

        def mask(hit):
            return jnp.concatenate([jnp.where(hit, 1.0, 0.0).astype(BF16)] * (bs // 16), axis=0)

        @pl.when(hub)
        def _():
            pl.semaphore_wait(barrier, n_fac + 1)

        @pl.when(core == 1)
        def _():
            pl.semaphore_wait(barrier, 1)

        t_sends = [
            pltpu.make_async_remote_copy(
                src_ref=t_ref.at[:, :, pl.ds(j * LANES, LANES)], dst_ref=mirror_t.at[j] if j < chunks - 1 else last_t,
                send_sem=t_send.at[j], recv_sem=t_recv.at[j], device_id=mirror, device_id_type=MESH)
            for j in range(chunks)
        ]
        order = [1, n_fac - 1] + list(range(2, n_fac - 1))
        f_sends = {
            k: [
                pltpu.make_async_remote_copy(
                    src_ref=src, dst_ref=dst.at[k], send_sem=f_send.at[k, i], recv_sem=f_recv.at[k, i],
                    device_id=fac_peer(k), device_id_type=MESH)
                for i, (src, dst) in enumerate(((dcol_ref, dc_land), (bcol_ref, bc_land), (land.at[0], land)))
            ]
            for k in order
        }
        passes = {
            k: [
                pltpu.make_async_remote_copy(
                    src_ref=dst.at[k], dst_ref=dst.at[k], send_sem=g_send.at[k, i], recv_sem=f_recv.at[k, i],
                    device_id=sibling, device_id_type=MESH)
                for i, dst in enumerate((dc_land, bc_land, land))
            ]
            for k in order
        }

        for send in t_sends:
            send.start()

        @pl.when(hub)
        def _():
            for k in order:
                for send in f_sends[k][:2]:
                    send.start()

        for i, ref in enumerate((d_in, b_in)):
            loads[i].wait()
            low = jnp.dot(ref[0:mid, :], to_low, preferred_element_type=F32)
            high = jnp.dot(ref[mid:v, :], to_high, preferred_element_type=F32)
            land[0, i] = (low + high).astype(BF16)

        def receive(k):
            for send in f_sends[k]:
                send.wait_recv()

            @pl.when(hub)
            def _():
                for send in passes[k]:
                    send.start()

        for load in loads[2:]:
            load.wait()

        for step, k in enumerate([0] + order):
            if step == 1:
                receive(order[0])
                receive(order[1])
            elif step == 2:
                for other in order[2:]:
                    receive(other)
            moves = [
                pltpu.make_async_copy(src.at[k], dst.at[k], local_sem.at[5 + i])
                for i, (src, dst) in enumerate(((dc_land, dc_s), (bc_land, bc_s)))
            ]
            for move in moves:
                move.start()

            twice = jnp.dot(land[k, 0], spread, preferred_element_type=F32).astype(BF16)
            none = jnp.zeros((bs, LANES), BF16)
            for r in range(nblk):
                h, i = divmod(r * bs, mid)
                part = twice[i:i + bs, h * LANES:(h + 1) * LANES]
                at = r % per * bs // LANES
                for side in range(GROUP // LANES):
                    piece = part * mask(which == r * bs % LANES // bs) if side == at else none
                    d_diag[k, r * bs:(r + 1) * bs, side * LANES:(side + 1) * LANES] = piece

            if step == 0:
                @pl.when(hub)
                def _():
                    for other in order:
                        f_sends[other][2].start()

            for move in moves:
                move.wait()
            twice = jnp.dot(land[k, 1], spread, preferred_element_type=F32).astype(BF16)
            for c in range(nblk):
                h, i = divmod(c * bs, mid)
                part = twice[i:i + bs, h * LANES:(h + 1) * LANES]
                col = bc_s[k, 0, c]
                for j in range(chunks):
                    piece = part * mask(which + (LANES // bs) * j == col)
                    (b_dense.at[j] if j < chunks - 1 else b_last)[c * bs:(c + 1) * bs, k * LANES:(k + 1) * LANES] = piece

            for g in range(groups):
                rows = slice(g * GROUP, (g + 1) * GROUP)
                picked = jnp.concatenate([own_t[dc_s[k, 0, g * per + i]] for i in range(per)], axis=0)
                left[rows, :] = jnp.dot(d_diag[k, rows, :], picked, preferred_element_type=F32).astype(BF16)

            right = jnp.concatenate(
                [b_dense[j, :, k * LANES:(k + 1) * LANES] for j in range(chunks - 1)]
                + [b_last[:, k * LANES:(k + 1) * LANES]], axis=1)
            part = lax.dot_general(left[...], right, NT, preferred_element_type=F32)
            if step == 0:
                acc[...] = part
            elif step < n_fac - 1:
                acc[...] += part
            else:
                acc[...] = (acc[...] + part).astype(BF16).astype(F32)

        def mirror_left(source):
            for k in range(n_fac):
                for g in range(groups):
                    rows = slice(g * GROUP, (g + 1) * GROUP)
                    picked = jnp.concatenate([source[dc_s[k, 0, g * per + i]] for i in range(per)], axis=0)
                    left_k[rows, k * LANES:(k + 1) * LANES] = jnp.dot(
                        d_diag[k, rows, :], picked, preferred_element_type=F32).astype(BF16)


        def mirror_step(j, _):
            pltpu.make_async_remote_copy(
                src_ref=t_ref.at[:, :, pl.ds(0, LANES)], dst_ref=mirror_t.at[j],
                send_sem=t_send.at[j], recv_sem=t_recv.at[j], device_id=mirror, device_id_type=MESH).wait_recv()
            work_t[...] = mirror_t[j]
            mirror_left(work_t)
            acc[...] += lax.dot_general(b_dense[j], left_k[...], NT, preferred_element_type=F32)
            return 0

        lax.fori_loop(0, chunks - 1, mirror_step, 0)
        t_sends[-1].wait_recv()
        mirror_left(last_t)
        for send in t_sends:
            send.wait_send()

        @pl.when(hub)
        def _():
            for k in order:
                for send in f_sends[k] + passes[k]:
                    send.wait_send()

    return kernel


def finish(acc, left_k, b_last, out_ref, stage, sem):
    v = acc.shape[1]
    half = v // 2
    blocks = [(0, half, 0), (half, half, 0), (0, half, half), (half, half // 2, half), (v - half // 2, half // 2, half)]
    copies = []
    for i, (m, rows, n) in enumerate(blocks):
        at = (slice(m, m + rows), slice(n, n + half))
        part = lax.dot_general(b_last[at[0], :], left_k[at[1], :], NT, preferred_element_type=F32)
        stage[at] = (acc[at] + part).astype(BF16)
        copy = pltpu.make_async_copy(stage.at[at], out_ref.at[at], sem.at[i])
        copy.start()
        copies.append(copy)
    for copy in copies:
        copy.wait()


def shards(amplitudes, mirror_slot, d_values, d_cols, b_values, b_cols):
    n_pair, n_fac = lax.axis_size("pair"), lax.axis_size("fac")
    v = amplitudes.shape[1]
    bs = d_values.shape[-1]
    nblk = v // bs
    chunks = v // LANES
    anywhere = pl.BlockSpec(memory_space=pltpu.HBM)
    parts = pl.pallas_call(
        make_kernel(n_pair, n_fac, v, bs),
        out_shape=(
            pltpu.VMEM((v, v), F32),
            pltpu.VMEM((v, n_fac * LANES), BF16),
            pltpu.VMEM((v, n_fac * LANES), BF16),
        ),
        in_specs=[anywhere] * 5,
        out_specs=[pl.BlockSpec(memory_space=pltpu.VMEM)] * 3,
        scratch_shapes=[
            pltpu.VMEM((nblk, bs, v), BF16),
            pltpu.VMEM((chunks - 1, nblk, bs, LANES), BF16),
            pltpu.VMEM((nblk, bs, LANES), BF16),
            pltpu.VMEM((nblk, bs, LANES), BF16),
            pltpu.VMEM((v, bs), BF16),
            pltpu.VMEM((v, bs), BF16),
            pltpu.VMEM((n_fac, 2, v // 2, LANES), BF16),
            pltpu.VMEM((n_fac, 1, nblk), jnp.int32),
            pltpu.VMEM((n_fac, 1, nblk), jnp.int32),
            pltpu.SMEM((n_fac, 1, nblk), jnp.int32),
            pltpu.SMEM((n_fac, 1, nblk), jnp.int32),
            pltpu.VMEM((n_fac, v, GROUP), BF16),
            pltpu.VMEM((chunks - 1, v, n_fac * LANES), BF16),
            pltpu.VMEM((v, v), BF16),
            pltpu.SemaphoreType.DMA((chunks,)),
            pltpu.SemaphoreType.DMA((chunks,)),
            pltpu.SemaphoreType.DMA((n_fac, 3)),
            pltpu.SemaphoreType.DMA((n_fac, 3)),
            pltpu.SemaphoreType.DMA((n_fac, 3)),
            pltpu.SemaphoreType.DMA((7,)),
        ],
        compiler_params=pltpu.CompilerParams(
            collective_id=0, has_side_effects=True, vmem_limit_bytes=40 * 2**20),
        name="ladder",
    )(*(
        pltpu.with_memory_space_constraint(x, pltpu.HBM)
        for x in (amplitudes.reshape(nblk, bs, v), d_values.reshape(v, bs), d_cols, b_values.reshape(v, bs), b_cols)
    ))
    out = pl.pallas_call(
        finish,
        out_shape=jax.ShapeDtypeStruct((v, v), BF16),
        in_specs=[pl.BlockSpec(memory_space=pltpu.VMEM)] * 3,
        out_specs=pl.BlockSpec(memory_space=pl.ANY),
        scratch_shapes=[pltpu.VMEM((v, v), BF16), pltpu.SemaphoreType.DMA((5,))],
        compiler_params=pltpu.CompilerParams(vmem_limit_bytes=40 * 2**20),
        name="finish",
    )(*parts)
    return jnp.take(out[None], mirror_slot, axis=0, mode="clip")


def solution(mesh):
    placed = (
        P(("pair", "fac"), None, None),
        P(("pair", "fac")),
        P("fac", None, None, None),
        P("fac", None),
        P("fac", None, None, None),
        P("fac", None),
    )
    return jax.shard_map(
        shards,
        mesh=mesh,
        in_specs=placed,
        out_specs=P(("pair", "fac"), None, None),
        check_vma=False,
    )
```

```python
import jax
import jax.numpy as jnp
from jax import lax
from jax.experimental import pallas as pl
from jax.experimental.pallas import tpu as pltpu
from jax.sharding import PartitionSpec as P

MESH = pl.DeviceIdType.MESH
F32 = jnp.float32
BF16 = jnp.bfloat16
LANES = 128
GROUP = 256
NT = (((1,), (1,)), ((), ()))


def make_kernel(n_pair, n_fac, v, bs):
    nblk = v // bs
    chunks = v // LANES
    groups = v // GROUP
    per = GROUP // bs
    half = n_pair // 2

    def kernel(
        t_ref, d_ref, dcol_ref, b_ref, bcol_ref, acc, left_k, b_last,
        own_t, mirror_t, work_t, last_t, d_in, b_in, land, dc_land, bc_land, dc_s, bc_s,
        d_diag, b_dense, left,
        t_send, t_recv, f_send, f_recv, g_send, local_sem,
    ):
        p = lax.axis_index("pair")
        f = lax.axis_index("fac")
        mirror = (lax.rem(p + half, n_pair), f)

        def fac_peer(k):
            return (p, lax.rem(f + n_fac - k, n_fac))

        core = lax.rem(p, 2)
        sibling = (p + 1 - 2 * core, f)
        hub = core == 0

        barrier = pltpu.get_barrier_semaphore()
        pl.semaphore_signal(barrier, inc=1, device_id=mirror, device_id_type=MESH)

        @pl.when(hub)
        def _():
            for k in range(1, n_fac):
                pl.semaphore_signal(barrier, inc=1, device_id=fac_peer(k), device_id_type=MESH)

        @pl.when(core == 1)
        def _():
            pl.semaphore_signal(barrier, inc=1, device_id=sibling, device_id_type=MESH)

        pairs = ((d_ref, d_in), (b_ref, b_in), (dcol_ref, dc_land.at[0]), (bcol_ref, bc_land.at[0]),
                 (t_ref, own_t))
        loads = [pltpu.make_async_copy(src, dst, local_sem.at[i]) for i, (src, dst) in enumerate(pairs)]
        for load in loads:
            load.start()

        lower = lax.broadcasted_iota(jnp.int32, (bs, LANES), 1) - lax.broadcasted_iota(jnp.int32, (bs, LANES), 0)
        to_low = jnp.where(lower == 0, 1.0, 0.0).astype(BF16)
        to_high = jnp.where(lower == bs, 1.0, 0.0).astype(BF16)
        from_i = lax.broadcasted_iota(jnp.int32, (LANES, GROUP), 0)
        to_i = lax.broadcasted_iota(jnp.int32, (LANES, GROUP), 1)
        spread = jnp.where(to_i // LANES * bs + lax.rem(to_i, bs) == from_i, 1.0, 0.0).astype(BF16)
        which = lax.broadcasted_iota(jnp.int32, (16, LANES), 1) // bs
        mid = v // 2

        def mask(hit):
            return jnp.concatenate([jnp.where(hit, 1.0, 0.0).astype(BF16)] * (bs // 16), axis=0)

        @pl.when(hub)
        def _():
            pl.semaphore_wait(barrier, n_fac + 1)

        @pl.when(core == 1)
        def _():
            pl.semaphore_wait(barrier, 1)

        t_sends = [
            pltpu.make_async_remote_copy(
                src_ref=t_ref.at[:, :, pl.ds(j * LANES, LANES)], dst_ref=mirror_t.at[j] if j < chunks - 1 else last_t,
                send_sem=t_send.at[j], recv_sem=t_recv.at[j], device_id=mirror, device_id_type=MESH)
            for j in range(chunks)
        ]
        order = [1, n_fac - 1] + list(range(2, n_fac - 1))
        f_sends = {
            k: [
                pltpu.make_async_remote_copy(
                    src_ref=src, dst_ref=dst.at[k], send_sem=f_send.at[k, i], recv_sem=f_recv.at[k, i],
                    device_id=fac_peer(k), device_id_type=MESH)
                for i, (src, dst) in enumerate(((dcol_ref, dc_land), (bcol_ref, bc_land), (land.at[0], land)))
            ]
            for k in order
        }
        passes = {
            k: [
                pltpu.make_async_remote_copy(
                    src_ref=dst.at[k], dst_ref=dst.at[k], send_sem=g_send.at[k, i], recv_sem=f_recv.at[k, i],
                    device_id=sibling, device_id_type=MESH)
                for i, dst in enumerate((dc_land, bc_land, land))
            ]
            for k in order
        }

        for send in t_sends[:-1]:
            send.start()

        @pl.when(hub)
        def _():
            t_sends[-1].start()

        @pl.when(hub)
        def _():
            for k in order:
                for send in f_sends[k][:2]:
                    send.start()

        for i, ref in enumerate((d_in, b_in)):
            loads[i].wait()
            low = jnp.dot(ref[0:mid, :], to_low, preferred_element_type=F32)
            high = jnp.dot(ref[mid:v, :], to_high, preferred_element_type=F32)
            land[0, i] = (low + high).astype(BF16)

        def receive(k):
            for send in f_sends[k]:
                send.wait_recv()

            @pl.when(hub)
            def _():
                for send in passes[k]:
                    send.start()

        for load in loads[2:]:
            load.wait()

        for step, k in enumerate([0] + order):
            if step == 1:
                receive(order[0])
                receive(order[1])
            elif step == 2:
                for other in order[2:]:
                    receive(other)
            moves = [
                pltpu.make_async_copy(src.at[k], dst.at[k], local_sem.at[5 + i])
                for i, (src, dst) in enumerate(((dc_land, dc_s), (bc_land, bc_s)))
            ]
            for move in moves:
                move.start()

            twice = jnp.dot(land[k, 0], spread, preferred_element_type=F32).astype(BF16)
            none = jnp.zeros((bs, LANES), BF16)
            for r in range(nblk):
                h, i = divmod(r * bs, mid)
                part = twice[i:i + bs, h * LANES:(h + 1) * LANES]
                at = r % per * bs // LANES
                for side in range(GROUP // LANES):
                    piece = part * mask(which == r * bs % LANES // bs) if side == at else none
                    d_diag[k, r * bs:(r + 1) * bs, side * LANES:(side + 1) * LANES] = piece

            if step == 0:
                @pl.when(hub)
                def _():
                    for other in order:
                        f_sends[other][2].start()

            for move in moves:
                move.wait()
            twice = jnp.dot(land[k, 1], spread, preferred_element_type=F32).astype(BF16)
            for c in range(nblk):
                h, i = divmod(c * bs, mid)
                part = twice[i:i + bs, h * LANES:(h + 1) * LANES]
                col = bc_s[k, 0, c]
                for j in range(chunks):
                    piece = part * mask(which + (LANES // bs) * j == col)
                    (b_dense.at[j] if j < chunks - 1 else b_last)[c * bs:(c + 1) * bs, k * LANES:(k + 1) * LANES] = piece

            for g in range(groups):
                rows = slice(g * GROUP, (g + 1) * GROUP)
                picked = jnp.concatenate([own_t[dc_s[k, 0, g * per + i]] for i in range(per)], axis=0)
                left[rows, :] = jnp.dot(d_diag[k, rows, :], picked, preferred_element_type=F32).astype(BF16)

            right = jnp.concatenate(
                [b_dense[j, :, k * LANES:(k + 1) * LANES] for j in range(chunks - 1)]
                + [b_last[:, k * LANES:(k + 1) * LANES]], axis=1)
            part = lax.dot_general(left[...], right, NT, preferred_element_type=F32)
            if step == 0:
                acc[...] = part
            elif step < n_fac - 1:
                acc[...] += part
            else:
                acc[...] = (acc[...] + part).astype(BF16).astype(F32)

        def mirror_left(source):
            for k in range(n_fac):
                for g in range(groups):
                    rows = slice(g * GROUP, (g + 1) * GROUP)
                    picked = jnp.concatenate([source[dc_s[k, 0, g * per + i]] for i in range(per)], axis=0)
                    left_k[rows, k * LANES:(k + 1) * LANES] = jnp.dot(
                        d_diag[k, rows, :], picked, preferred_element_type=F32).astype(BF16)


        def mirror_step(j, _):
            pltpu.make_async_remote_copy(
                src_ref=t_ref.at[:, :, pl.ds(0, LANES)], dst_ref=mirror_t.at[j],
                send_sem=t_send.at[j], recv_sem=t_recv.at[j], device_id=mirror, device_id_type=MESH).wait_recv()

            @pl.when(jnp.logical_and(core == 1, j == chunks - 2))
            def _():
                t_sends[-1].start()

            work_t[...] = mirror_t[j]
            mirror_left(work_t)
            acc[...] += lax.dot_general(b_dense[j], left_k[...], NT, preferred_element_type=F32)
            return 0

        lax.fori_loop(0, chunks - 1, mirror_step, 0)
        t_sends[-1].wait_recv()
        mirror_left(last_t)
        for send in t_sends:
            send.wait_send()

        @pl.when(hub)
        def _():
            for k in order:
                for send in f_sends[k] + passes[k]:
                    send.wait_send()

    return kernel


def finish(acc, left_k, b_last, out_ref, stage, sem):
    v = acc.shape[1]
    half = v // 2
    blocks = [(0, half, 0), (half, half, 0), (0, half, half), (half, half // 2, half), (v - half // 2, half // 2, half)]
    copies = []
    for i, (m, rows, n) in enumerate(blocks):
        at = (slice(m, m + rows), slice(n, n + half))
        part = lax.dot_general(b_last[at[0], :], left_k[at[1], :], NT, preferred_element_type=F32)
        stage[at] = (acc[at] + part).astype(BF16)
        copy = pltpu.make_async_copy(stage.at[at], out_ref.at[at], sem.at[i])
        copy.start()
        copies.append(copy)
    for copy in copies:
        copy.wait()


def shards(amplitudes, mirror_slot, d_values, d_cols, b_values, b_cols):
    n_pair, n_fac = lax.axis_size("pair"), lax.axis_size("fac")
    v = amplitudes.shape[1]
    bs = d_values.shape[-1]
    nblk = v // bs
    chunks = v // LANES
    anywhere = pl.BlockSpec(memory_space=pltpu.HBM)
    parts = pl.pallas_call(
        make_kernel(n_pair, n_fac, v, bs),
        out_shape=(
            pltpu.VMEM((v, v), F32),
            pltpu.VMEM((v, n_fac * LANES), BF16),
            pltpu.VMEM((v, n_fac * LANES), BF16),
        ),
        in_specs=[anywhere] * 5,
        out_specs=[pl.BlockSpec(memory_space=pltpu.VMEM)] * 3,
        scratch_shapes=[
            pltpu.VMEM((nblk, bs, v), BF16),
            pltpu.VMEM((chunks - 1, nblk, bs, LANES), BF16),
            pltpu.VMEM((nblk, bs, LANES), BF16),
            pltpu.VMEM((nblk, bs, LANES), BF16),
            pltpu.VMEM((v, bs), BF16),
            pltpu.VMEM((v, bs), BF16),
            pltpu.VMEM((n_fac, 2, v // 2, LANES), BF16),
            pltpu.VMEM((n_fac, 1, nblk), jnp.int32),
            pltpu.VMEM((n_fac, 1, nblk), jnp.int32),
            pltpu.SMEM((n_fac, 1, nblk), jnp.int32),
            pltpu.SMEM((n_fac, 1, nblk), jnp.int32),
            pltpu.VMEM((n_fac, v, GROUP), BF16),
            pltpu.VMEM((chunks - 1, v, n_fac * LANES), BF16),
            pltpu.VMEM((v, v), BF16),
            pltpu.SemaphoreType.DMA((chunks,)),
            pltpu.SemaphoreType.DMA((chunks,)),
            pltpu.SemaphoreType.DMA((n_fac, 3)),
            pltpu.SemaphoreType.DMA((n_fac, 3)),
            pltpu.SemaphoreType.DMA((n_fac, 3)),
            pltpu.SemaphoreType.DMA((7,)),
        ],
        compiler_params=pltpu.CompilerParams(
            collective_id=0, has_side_effects=True, vmem_limit_bytes=40 * 2**20),
        name="ladder",
    )(*(
        pltpu.with_memory_space_constraint(x, pltpu.HBM)
        for x in (amplitudes.reshape(nblk, bs, v), d_values.reshape(v, bs), d_cols, b_values.reshape(v, bs), b_cols)
    ))
    out = pl.pallas_call(
        finish,
        out_shape=jax.ShapeDtypeStruct((v, v), BF16),
        in_specs=[pl.BlockSpec(memory_space=pltpu.VMEM)] * 3,
        out_specs=pl.BlockSpec(memory_space=pl.ANY),
        scratch_shapes=[pltpu.VMEM((v, v), BF16), pltpu.SemaphoreType.DMA((5,))],
        compiler_params=pltpu.CompilerParams(vmem_limit_bytes=40 * 2**20),
        name="finish",
    )(*parts)
    return jnp.take(out[None], mirror_slot, axis=0, mode="clip")


def solution(mesh):
    placed = (
        P(("pair", "fac"), None, None),
        P(("pair", "fac")),
        P("fac", None, None, None),
        P("fac", None),
        P("fac", None, None, None),
        P("fac", None),
    )
    return jax.shard_map(
        shards,
        mesh=mesh,
        in_specs=placed,
        out_specs=P(("pair", "fac"), None, None),
        check_vma=False,
    )
```

```python
import jax
import jax.numpy as jnp
from jax import lax
from jax.experimental import pallas as pl
from jax.experimental.pallas import tpu as pltpu
from jax.sharding import PartitionSpec as P

MESH = pl.DeviceIdType.MESH
F32 = jnp.float32
BF16 = jnp.bfloat16
LANES = 128
GROUP = 256
NT = (((1,), (1,)), ((), ()))


def make_kernel(n_pair, n_fac, v, bs):
    nblk = v // bs
    chunks = v // LANES
    groups = v // GROUP
    per = GROUP // bs
    half = n_pair // 2

    def kernel(
        t_ref, d_ref, dcol_ref, b_ref, bcol_ref, acc, left_k, b_last,
        own_t, mirror_t, work_t, last_t, d_in, b_in, land, dc_land, bc_land, dc_s, bc_s,
        d_diag, b_dense, left,
        t_send, t_recv, f_send, f_recv, g_send, local_sem,
    ):
        p = lax.axis_index("pair")
        f = lax.axis_index("fac")
        mirror = (lax.rem(p + half, n_pair), f)

        def fac_peer(k):
            return (p, lax.rem(f + n_fac - k, n_fac))

        core = lax.rem(p, 2)
        sibling = (p + 1 - 2 * core, f)
        hub = core == 0

        barrier = pltpu.get_barrier_semaphore()
        pl.semaphore_signal(barrier, inc=1, device_id=mirror, device_id_type=MESH)

        @pl.when(hub)
        def _():
            for k in range(1, n_fac):
                pl.semaphore_signal(barrier, inc=1, device_id=fac_peer(k), device_id_type=MESH)

        @pl.when(core == 1)
        def _():
            pl.semaphore_signal(barrier, inc=1, device_id=sibling, device_id_type=MESH)

        pairs = ((d_ref, d_in), (b_ref, b_in), (dcol_ref, dc_land.at[0]), (bcol_ref, bc_land.at[0]),
                 (t_ref, own_t))
        loads = [pltpu.make_async_copy(src, dst, local_sem.at[i]) for i, (src, dst) in enumerate(pairs)]
        for load in loads:
            load.start()

        lower = lax.broadcasted_iota(jnp.int32, (bs, LANES), 1) - lax.broadcasted_iota(jnp.int32, (bs, LANES), 0)
        to_low = jnp.where(lower == 0, 1.0, 0.0).astype(BF16)
        to_high = jnp.where(lower == bs, 1.0, 0.0).astype(BF16)
        from_i = lax.broadcasted_iota(jnp.int32, (LANES, GROUP), 0)
        to_i = lax.broadcasted_iota(jnp.int32, (LANES, GROUP), 1)
        spread = jnp.where(to_i // LANES * bs + lax.rem(to_i, bs) == from_i, 1.0, 0.0).astype(BF16)
        which = lax.broadcasted_iota(jnp.int32, (16, LANES), 1) // bs
        mid = v // 2

        def mask(hit):
            return jnp.concatenate([jnp.where(hit, 1.0, 0.0).astype(BF16)] * (bs // 16), axis=0)

        @pl.when(hub)
        def _():
            pl.semaphore_wait(barrier, n_fac + 1)

        @pl.when(core == 1)
        def _():
            pl.semaphore_wait(barrier, 1)

        t_sends = [
            pltpu.make_async_remote_copy(
                src_ref=t_ref.at[:, :, pl.ds(j * LANES, LANES)], dst_ref=mirror_t.at[j] if j < chunks - 1 else last_t,
                send_sem=t_send.at[j], recv_sem=t_recv.at[j], device_id=mirror, device_id_type=MESH)
            for j in range(chunks)
        ]
        order = [1, n_fac - 1] + list(range(2, n_fac - 1))
        f_sends = {
            k: [
                pltpu.make_async_remote_copy(
                    src_ref=src, dst_ref=dst.at[k], send_sem=f_send.at[k, i], recv_sem=f_recv.at[k, i],
                    device_id=fac_peer(k), device_id_type=MESH)
                for i, (src, dst) in enumerate(((dcol_ref, dc_land), (bcol_ref, bc_land), (land.at[0], land)))
            ]
            for k in order
        }
        passes = {
            k: [
                pltpu.make_async_remote_copy(
                    src_ref=dst.at[k], dst_ref=dst.at[k], send_sem=g_send.at[k, i], recv_sem=f_recv.at[k, i],
                    device_id=sibling, device_id_type=MESH)
                for i, dst in enumerate((dc_land, bc_land, land))
            ]
            for k in order
        }

        for send in t_sends[:-1]:
            send.start()

        @pl.when(hub)
        def _():
            t_sends[-1].start()

        @pl.when(hub)
        def _():
            for k in order:
                for send in f_sends[k][:2]:
                    send.start()

        for i, ref in enumerate((d_in, b_in)):
            loads[i].wait()
            low = jnp.dot(ref[0:mid, :], to_low, preferred_element_type=F32)
            high = jnp.dot(ref[mid:v, :], to_high, preferred_element_type=F32)
            land[0, i] = (low + high).astype(BF16)

        def receive(k):
            for send in f_sends[k]:
                send.wait_recv()

            @pl.when(hub)
            def _():
                for send in passes[k]:
                    send.start()

        for load in loads[2:]:
            load.wait()

        for step, k in enumerate([0] + order):
            if step == 1:
                receive(order[0])
                receive(order[1])
            elif step == 2:
                for other in order[2:]:
                    receive(other)
            moves = [
                pltpu.make_async_copy(src.at[k], dst.at[k], local_sem.at[5 + i])
                for i, (src, dst) in enumerate(((dc_land, dc_s), (bc_land, bc_s)))
            ]
            for move in moves:
                move.start()

            twice = jnp.dot(land[k, 0], spread, preferred_element_type=F32).astype(BF16)
            none = jnp.zeros((bs, LANES), BF16)
            for r in range(nblk):
                h, i = divmod(r * bs, mid)
                part = twice[i:i + bs, h * LANES:(h + 1) * LANES]
                at = r % per * bs // LANES
                for side in range(GROUP // LANES):
                    piece = part * mask(which == r * bs % LANES // bs) if side == at else none
                    d_diag[k, r * bs:(r + 1) * bs, side * LANES:(side + 1) * LANES] = piece

            if step == 0:
                @pl.when(hub)
                def _():
                    for other in order:
                        f_sends[other][2].start()

            for move in moves:
                move.wait()
            twice = jnp.dot(land[k, 1], spread, preferred_element_type=F32).astype(BF16)
            for c in range(nblk):
                h, i = divmod(c * bs, mid)
                part = twice[i:i + bs, h * LANES:(h + 1) * LANES]
                col = bc_s[k, 0, c]
                for j in range(chunks):
                    piece = part * mask(which + (LANES // bs) * j == col)
                    (b_dense.at[j] if j < chunks - 1 else b_last)[c * bs:(c + 1) * bs, k * LANES:(k + 1) * LANES] = piece

            for g in range(groups):
                rows = slice(g * GROUP, (g + 1) * GROUP)
                picked = jnp.concatenate([own_t[dc_s[k, 0, g * per + i]] for i in range(per)], axis=0)
                left[rows, :] = jnp.dot(d_diag[k, rows, :], picked, preferred_element_type=F32).astype(BF16)

            right = jnp.concatenate(
                [b_dense[j, :, k * LANES:(k + 1) * LANES] for j in range(chunks - 1)]
                + [b_last[:, k * LANES:(k + 1) * LANES]], axis=1)
            part = lax.dot_general(left[...], right, NT, preferred_element_type=F32)
            if step == 0:
                acc[...] = part
            elif step < n_fac - 1:
                acc[...] += part
            else:
                acc[...] = (acc[...] + part).astype(BF16).astype(F32)

        def mirror_left(source):
            for k in range(n_fac):
                for g in range(groups):
                    rows = slice(g * GROUP, (g + 1) * GROUP)
                    picked = jnp.concatenate([source[dc_s[k, 0, g * per + i]] for i in range(per)], axis=0)
                    left_k[rows, k * LANES:(k + 1) * LANES] = jnp.dot(
                        d_diag[k, rows, :], picked, preferred_element_type=F32).astype(BF16)


        def mirror_step(j, _):
            @pl.when(jnp.logical_and(core == 1, j == chunks - 2))
            def _():
                t_sends[-2].wait_send()
                t_sends[-1].start()

            pltpu.make_async_remote_copy(
                src_ref=t_ref.at[:, :, pl.ds(0, LANES)], dst_ref=mirror_t.at[j],
                send_sem=t_send.at[j], recv_sem=t_recv.at[j], device_id=mirror, device_id_type=MESH).wait_recv()
            work_t[...] = mirror_t[j]
            mirror_left(work_t)
            acc[...] += lax.dot_general(b_dense[j], left_k[...], NT, preferred_element_type=F32)
            return 0

        lax.fori_loop(0, chunks - 1, mirror_step, 0)
        t_sends[-1].wait_recv()
        mirror_left(last_t)
        for send in t_sends[:-2] + t_sends[-1:]:
            send.wait_send()

        @pl.when(hub)
        def _():
            t_sends[-2].wait_send()
            for k in order:
                for send in f_sends[k] + passes[k]:
                    send.wait_send()

    return kernel


def finish(acc, left_k, b_last, out_ref, stage, sem):
    v = acc.shape[1]
    half = v // 2
    blocks = [(0, half, 0), (half, half, 0), (0, half, half), (half, half // 2, half), (v - half // 2, half // 2, half)]
    copies = []
    for i, (m, rows, n) in enumerate(blocks):
        at = (slice(m, m + rows), slice(n, n + half))
        part = lax.dot_general(b_last[at[0], :], left_k[at[1], :], NT, preferred_element_type=F32)
        stage[at] = (acc[at] + part).astype(BF16)
        copy = pltpu.make_async_copy(stage.at[at], out_ref.at[at], sem.at[i])
        copy.start()
        copies.append(copy)
    for copy in copies:
        copy.wait()


def shards(amplitudes, mirror_slot, d_values, d_cols, b_values, b_cols):
    n_pair, n_fac = lax.axis_size("pair"), lax.axis_size("fac")
    v = amplitudes.shape[1]
    bs = d_values.shape[-1]
    nblk = v // bs
    chunks = v // LANES
    anywhere = pl.BlockSpec(memory_space=pltpu.HBM)
    parts = pl.pallas_call(
        make_kernel(n_pair, n_fac, v, bs),
        out_shape=(
            pltpu.VMEM((v, v), F32),
            pltpu.VMEM((v, n_fac * LANES), BF16),
            pltpu.VMEM((v, n_fac * LANES), BF16),
        ),
        in_specs=[anywhere] * 5,
        out_specs=[pl.BlockSpec(memory_space=pltpu.VMEM)] * 3,
        scratch_shapes=[
            pltpu.VMEM((nblk, bs, v), BF16),
            pltpu.VMEM((chunks - 1, nblk, bs, LANES), BF16),
            pltpu.VMEM((nblk, bs, LANES), BF16),
            pltpu.VMEM((nblk, bs, LANES), BF16),
            pltpu.VMEM((v, bs), BF16),
            pltpu.VMEM((v, bs), BF16),
            pltpu.VMEM((n_fac, 2, v // 2, LANES), BF16),
            pltpu.VMEM((n_fac, 1, nblk), jnp.int32),
            pltpu.VMEM((n_fac, 1, nblk), jnp.int32),
            pltpu.SMEM((n_fac, 1, nblk), jnp.int32),
            pltpu.SMEM((n_fac, 1, nblk), jnp.int32),
            pltpu.VMEM((n_fac, v, GROUP), BF16),
            pltpu.VMEM((chunks - 1, v, n_fac * LANES), BF16),
            pltpu.VMEM((v, v), BF16),
            pltpu.SemaphoreType.DMA((chunks,)),
            pltpu.SemaphoreType.DMA((chunks,)),
            pltpu.SemaphoreType.DMA((n_fac, 3)),
            pltpu.SemaphoreType.DMA((n_fac, 3)),
            pltpu.SemaphoreType.DMA((n_fac, 3)),
            pltpu.SemaphoreType.DMA((7,)),
        ],
        compiler_params=pltpu.CompilerParams(
            collective_id=0, has_side_effects=True, vmem_limit_bytes=40 * 2**20),
        name="ladder",
    )(*(
        pltpu.with_memory_space_constraint(x, pltpu.HBM)
        for x in (amplitudes.reshape(nblk, bs, v), d_values.reshape(v, bs), d_cols, b_values.reshape(v, bs), b_cols)
    ))
    out = pl.pallas_call(
        finish,
        out_shape=jax.ShapeDtypeStruct((v, v), BF16),
        in_specs=[pl.BlockSpec(memory_space=pltpu.VMEM)] * 3,
        out_specs=pl.BlockSpec(memory_space=pl.ANY),
        scratch_shapes=[pltpu.VMEM((v, v), BF16), pltpu.SemaphoreType.DMA((5,))],
        compiler_params=pltpu.CompilerParams(vmem_limit_bytes=40 * 2**20),
        name="finish",
    )(*parts)
    return jnp.take(out[None], mirror_slot, axis=0, mode="clip")


def solution(mesh):
    placed = (
        P(("pair", "fac"), None, None),
        P(("pair", "fac")),
        P("fac", None, None, None),
        P("fac", None),
        P("fac", None, None, None),
        P("fac", None),
    )
    return jax.shard_map(
        shards,
        mesh=mesh,
        in_specs=placed,
        out_specs=P(("pair", "fac"), None, None),
        check_vma=False,
    )
```
